256 devices in a mesh: ctx: 8 (over z), chan: 32 (over x, y, core).
Axes of the slice: x: 4, y: 4, z: 8, core: 2. Of those that a mesh axis runs over, the one named last changes fastest.
Arguments:
- query_rows: bfloat16 [2048, 8192], P('ctx', 'chan'), may hold values from -6 to 6
- key_rows: bfloat16 [2048, 8192], P('ctx', 'chan'), may hold values from -6 to 6
- value_rows: bfloat16 [2048, 8192], P('ctx', 'chan'), may hold values from -6 to 6
- short_taps: float32 [3, 3, 8192], P(None, None, 'chan'), may hold values from -3 to 3
- long_filter: bfloat16 [2048, 8192], P('ctx', 'chan'), may hold values from -4 to 4
- direction: bfloat16 [2048, 8192], P('ctx', 'chan'), may hold values from -4 to 4
- w_out: bfloat16 [8192, 8192], P('chan'), may hold values from -0.125 to 0.125
- target: bfloat16 [2048, 8192], P('ctx'), may hold values from -6 to 6
Outputs:
- grad_filter: float32 [2048, 8192], P('ctx', 'chan')
- hvp_filter: float32 [2048, 8192], P('ctx', 'chan')
The draws below stay inside these ranges and needn't reach their ends.
All inputs are finite; a program needn't handle non-finite values.
Results may differ from the reference program's by a relative error of at most 0.033.
Values may be sent and summed in bfloat16 or wider, within the bound.
A program may use at most 128 MiB of HBM per device.

```python
import math
import jax
import jax.numpy as jnp
from jax import lax

D = 8192
CH = 256
TOKENS = 2048


def filter_law(key, salt_value):
    folded = jax.random.fold_in(key, salt_value)
    key_amp, key_rate = jax.random.split(folded)
    lag_index = jnp.arange(TOKENS, dtype=jnp.float32)[:, None]
    amplitude = jnp.clip(jax.random.normal(key_amp, (TOKENS, D), jnp.float32), -4.0, 4.0)
    decay_rate = jnp.exp(jax.random.uniform(key_rate, (1, D), jnp.float32, math.log(0.5 / TOKENS), math.log(1.0 / 40.0)))
    energy = (1.0 - jnp.exp(-2.0 * decay_rate * TOKENS)) / (1.0 - jnp.exp(-2.0 * decay_rate))
    return amplitude * jnp.exp(-decay_rate * lag_index) / jnp.sqrt(energy)


def draw_long_filter(key, part):
    return filter_law(key, 11).astype(jnp.bfloat16)


def draw_direction(key, part):
    return filter_law(key, 23).astype(jnp.bfloat16)


def strengthened(entries, own_key, source, target, parts, factor):
    owner, partner = [(jnp.arange(entries.shape[position]) // (entries.shape[position] // parts)).reshape([-1 if axis == position else 1 for axis in range(entries.ndim)]) for position in (source, target)]
    chosen = jax.random.permutation(own_key, parts)[partner]
    strong = (owner == chosen) | (owner == (partner + parts // 2) % parts)
    return jnp.where(strong, factor * entries, entries)


def block_levels(key, shape, cuts, smallest, high):
    gain, own = 1.0, jax.random.fold_in(key, 6)
    for dim, parts in cuts:
        draws = jnp.exp(jax.random.uniform(jax.random.fold_in(own, dim), (parts,), jnp.float32, smallest / len(cuts), high / len(cuts)))
        gain = gain * jnp.repeat(draws, shape[dim] // parts).reshape([-1 if axis == dim else 1 for axis in range(len(shape))])
    return gain


def noise(own_key, shape, width, limit, shards=(), held_as=jnp.bfloat16):
    array = width * jax.random.normal(own_key, shape, jnp.float32)
    if shards:
        array = array * block_levels(own_key, shape, shards, -0.22, 0.18)
    return jnp.clip(array, -limit, limit).astype(held_as)


def bell_draw_with(key, shape, width, most, shards, heavy, kind=jnp.bfloat16):
    drawn = width * jax.random.normal(key, shape, jnp.float32)
    if shards:
        drawn = drawn * block_levels(key, shape, shards, -0.22, 0.18)
    return jnp.clip(strengthened(drawn, jax.random.fold_in(key, 3), *heavy), -most, most).astype(kind)


def setup_inputs(seed: int = 0) -> dict:
    arg_keys = jax.random.split(jax.random.key(seed), 9)
    return {
        "query_rows": noise(arg_keys[0], (TOKENS, D), 1.0, 6.0, ((0, 8), (1, 32))),
        "key_rows": noise(arg_keys[1], (TOKENS, D), 1.0, 6.0, ((0, 8), (1, 32))),
        "value_rows": noise(arg_keys[2], (TOKENS, D), 1.0, 6.0, ((0, 8), (1, 32))),
        "short_taps": noise(arg_keys[3], (3, 3, D), 0.6, 3.0, ((2, 32),), jnp.float32),
        "long_filter": draw_long_filter(jax.random.fold_in(arg_keys[8], 71), 0),
        "direction": draw_direction(jax.random.fold_in(arg_keys[8], 71), 0),
        "w_out": bell_draw_with(arg_keys[6], (D, D), D ** -0.5, 0.125, ((0, 32),), (0, 1, 32, 2.75)),
        "target": noise(arg_keys[7], (TOKENS, D), 1.5, 6.0, ((0, 8),)),
    }


def short_filtered(stream, coeffs):
    values = stream.astype(jnp.float32)
    padded = jnp.concatenate([jnp.zeros((2, values.shape[1]), jnp.float32), values], axis=0)
    length = values.shape[0]
    return coeffs[0] * padded[2:2 + length] + coeffs[1] * padded[1:1 + length] + coeffs[2] * padded[0:length]

def causal_conv(filter_rows, signal):
    length = filter_rows.shape[0]
    fft_len = 2 * length
    spectrum = jnp.fft.rfft(filter_rows.astype(jnp.float32), n=fft_len, axis=0) * jnp.fft.rfft(signal.astype(jnp.float32), n=fft_len, axis=0)
    return jnp.fft.irfft(spectrum, n=fft_len, axis=0)[:length].astype(jnp.float32)

def correlate(cotangent, signal):
    length = cotangent.shape[0]
    fft_len = 2 * length
    spectrum = jnp.fft.rfft(cotangent.astype(jnp.float32), n=fft_len, axis=0) * jnp.conj(jnp.fft.rfft(signal.astype(jnp.float32), n=fft_len, axis=0))
    return jnp.fft.irfft(spectrum, n=fft_len, axis=0)[:length].astype(jnp.float32)

def project(stacked, w_out):
    blocks = D // CH
    pieces = jnp.transpose(stacked.reshape(stacked.shape[0], blocks, CH), (1, 0, 2))
    weights = w_out.reshape(blocks, CH, D)

    def add_block(running, operands):
        product = jnp.dot(operands[0].astype(jnp.float32), operands[1].astype(jnp.float32), preferred_element_type=jnp.float32)
        rounded = lax.optimization_barrier(product.astype(jnp.bfloat16))
        return (running + rounded.astype(jnp.float32), None)
    summed, unused = lax.scan(add_block, jnp.zeros((stacked.shape[0], D), jnp.float32), (pieces, weights))
    return summed

def reference(query_rows, key_rows, value_rows, short_taps, long_filter, direction, w_out, target):
    gate_in = short_filtered(query_rows, short_taps[0])
    key_short = short_filtered(key_rows, short_taps[1])
    value_short = short_filtered(value_rows, short_taps[2])
    mixed_rows = (key_short * value_short).astype(jnp.bfloat16)
    convolved = causal_conv(long_filter, mixed_rows)
    convolved_dir = causal_conv(direction, mixed_rows)
    gated_rows = (gate_in * convolved).astype(jnp.bfloat16)
    gated_dir = (gate_in * convolved_dir).astype(jnp.bfloat16)
    summed = project(jnp.concatenate([gated_rows, gated_dir], axis=0), w_out)
    seq_total = query_rows.shape[0]
    scaling = 1.0 / math.sqrt(seq_total)
    bent_out = jnp.tanh(summed[:seq_total] - target.astype(jnp.float32))
    cot_grad = (scaling * bent_out).astype(jnp.bfloat16)
    cot_hvp = (scaling * (1.0 - bent_out * bent_out) * summed[seq_total:]).astype(jnp.bfloat16)
    cotangent = jnp.concatenate([cot_grad, cot_hvp], axis=0).astype(jnp.float32)
    backward = jnp.dot(cotangent, w_out.astype(jnp.float32).T, preferred_element_type=jnp.float32)
    dz_grad = (gate_in * backward[:seq_total]).astype(jnp.bfloat16)
    dz_hvp = (gate_in * backward[seq_total:]).astype(jnp.bfloat16)
    return (correlate(dz_grad, mixed_rows), correlate(dz_hvp, mixed_rows))
```

```python
import functools
import math

import jax
import jax.numpy as jnp
from jax import lax
from jax.experimental import pallas as pl
from jax.experimental.pallas import tpu as pltpu
from jax.sharding import PartitionSpec as P

MESH = pl.DeviceIdType.MESH
BF = jnp.bfloat16
F32 = jnp.float32
VM = pl.BlockSpec(memory_space=pltpu.VMEM)
ANY = pl.BlockSpec(memory_space=pl.ANY)
NZ = 8
NR = 4
BL = 256
LN = 128
CW = BL // NZ


class Copies:
    def __init__(self, send_sems, recv_sems):
        self.send_sems, self.recv_sems, self.made = send_sems, recv_sems, []

    def start(self, src, dst, device):
        slot = len(self.made)
        copy = pltpu.make_async_remote_copy(
            src_ref=src,
            dst_ref=dst,
            send_sem=self.send_sems.at[slot],
            recv_sem=self.recv_sems.at[slot],
            device_id=device,
            device_id_type=MESH,
        )
        copy.start()
        self.made.append(copy)
        return copy

    def drain(self):
        for copy in self.made:
            copy.wait_send()


def barrier(devices):
    sem = pltpu.get_barrier_semaphore()
    for device in devices:
        pl.semaphore_signal(sem, inc=1, device_id=device, device_id_type=MESH)
    pl.semaphore_wait(sem, len(devices))


def z_peers(z):
    return [{"ctx": lax.rem(z + off, NZ)} for off in range(1, NZ)]


def enter_kernel(
    q_ref, k_ref, v_ref, taps_ref, h_ref, d_ref, w_ref,
    gate_ref, got_ref, wp_ref,
    halo, ext, out_buf, in_buf, send_sems, recv_sems,
):
    z, c = lax.axis_index("ctx"), lax.axis_index("chan")
    core = lax.rem(c, 2)
    partner = {"chan": c + 1 - 2 * core}
    barrier(z_peers(z) + [partner])
    cp = Copies(send_sems, recv_sems)
    half = w_ref.shape[1] // 2
    after = {"ctx": lax.rem(z + 1, NZ)}
    halos = [
        cp.start(ref.at[pl.ds(BL - 16, 16)], halo.at[i], after)
        for i, ref in enumerate((q_ref, k_ref, v_ref))
    ]
    w_copy = cp.start(
        w_ref.at[:, pl.ds(pl.multiple_of((1 - core) * half, LN), half)], wp_ref, partner
    )

    def put(value, which):
        for jj in range(2):
            turned = value[jj * LN : (jj + 1) * LN].T
            out_buf[:, which, jj] = turned.reshape(NZ, CW, LN).astype(BF)

    put(h_ref[...].astype(F32), 0)
    put(d_ref[...].astype(F32), 1)
    arrivals = []
    for off in range(1, NZ):
        to = lax.rem(z + off, NZ)
        arrivals.append(
            cp.start(out_buf.at[to, pl.ds(0, 2)], in_buf.at[z, pl.ds(0, 2)], {"ctx": to})
        )
    for copy in halos:
        copy.wait_recv()
    inside = (z > 0).astype(F32)
    short = []
    for i, ref in enumerate((q_ref, k_ref, v_ref)):
        ext[i, pl.ds(0, 16)] = halo[i].astype(F32) * inside
        ext[i, pl.ds(16, BL)] = ref[...].astype(F32)
        short.append(
            taps_ref[pl.ds(3 * i, 1)] * ext[i, pl.ds(16, BL)]
            + taps_ref[pl.ds(3 * i + 1, 1)] * ext[i, pl.ds(15, BL)]
            + taps_ref[pl.ds(3 * i + 2, 1)] * ext[i, pl.ds(14, BL)]
        )
    gate_ref[...] = short[0]
    put(short[1] * short[2], 2)
    for off in range(1, NZ):
        to = lax.rem(z + off, NZ)
        arrivals.append(cp.start(out_buf.at[to, 2], in_buf.at[z, 2], {"ctx": to}))
    in_buf[z] = out_buf[z]
    for copy in arrivals:
        copy.wait_recv()
    got_ref[...] = in_buf[...]
    w_copy.wait_recv()
    cp.drain()


def enter(q, k, v, taps, h, d, w):
    return pl.pallas_call(
        enter_kernel,
        out_shape=(
            jax.ShapeDtypeStruct((BL, BL), F32),
            jax.ShapeDtypeStruct((NZ, 3, 2, CW, LN), BF),
            jax.ShapeDtypeStruct((BL, w.shape[1] // 2), BF),
        ),
        in_specs=[VM] * 6 + [ANY],
        out_specs=(VM, VM, ANY),
        scratch_shapes=[
            pltpu.VMEM((3, 16, BL), BF),
            pltpu.VMEM((3, BL + 16, BL), F32),
            pltpu.VMEM((NZ, 3, 2, CW, LN), BF),
            pltpu.VMEM((NZ, 3, 2, CW, LN), BF),
            pltpu.SemaphoreType.DMA((18,)),
            pltpu.SemaphoreType.DMA((18,)),
        ],
        compiler_params=pltpu.CompilerParams(collective_id=0, has_side_effects=True),
        name="enter",
    )(q, k, v, taps, h, d, w)


def toeplitz(m_buf, channel):
    row = lax.broadcasted_iota(jnp.int32, (LN, LN), 0)
    lane = lax.broadcasted_iota(jnp.int32, (LN, LN), 1)
    keep = lane >= row
    before = jnp.zeros((LN, LN), F32)
    pieces = []
    for piece in range(2 * NZ):
        line = m_buf[pl.ds(piece * CW + channel, 1)]
        turned = pltpu.roll(
            jnp.broadcast_to(line, (LN, LN)), 0, 1, stride=1, stride_axis=0
        )
        pieces.append(jnp.where(keep, turned, before).astype(BF))
        before = turned
    return pieces


def conv_kernel(backward, m_at, x_at, m_ref, x_ref, y_ref, m_buf, x_buf, y_buf):
    n = 2 * NZ
    rows = n * CW
    zero_at, data_at = (rows, 0) if backward else (0, rows)
    for sig in range(2):
        x_buf[sig, pl.ds(zero_at, rows)] = jnp.zeros((rows, LN), F32)
        for src in range(NZ):
            for jj in range(2):
                x_buf[sig, pl.ds(data_at + (2 * src + jj) * CW, CW)] = x_ref[
                    src, x_at + sig, jj
                ].astype(F32)
    for src in range(NZ):
        for jj in range(2):
            m_buf[pl.ds((2 * src + jj) * CW, CW)] = m_ref[src, m_at, jj].astype(F32)

    def one(channel, carry):
        pieces = toeplitz(m_buf, channel)
        lines = []
        for k in range(n):
            first = (k if backward else n - k) * CW + channel
            lines.append(
                jnp.concatenate(
                    [x_buf[sig, pl.ds(first, n, stride=CW)] for sig in range(2)], axis=0
                ).astype(BF)
            )
        left = jnp.concatenate(lines, axis=1)
        if backward:
            y = lax.dot_general(
                left,
                jnp.concatenate(pieces, axis=1),
                (((1,), (1,)), ((), ())),
                preferred_element_type=F32,
            )
        else:
            y = jnp.dot(left, jnp.concatenate(pieces, axis=0), preferred_element_type=F32)
        for sig in range(2):
            y_buf[sig, pl.ds(channel, n, stride=CW)] = y[sig * n : (sig + 1) * n]
        return carry

    lax.fori_loop(0, CW, one, 0)
    for dest in range(NZ):
        for sig in range(2):
            for jj in range(2):
                y_ref[dest, sig, jj] = y_buf[sig, pl.ds((2 * dest + jj) * CW, CW)].astype(BF)


def convolve(backward, m_at, x_at, m, x):
    rows = 2 * NZ * CW
    return pl.pallas_call(
        functools.partial(conv_kernel, backward, m_at, x_at),
        out_shape=jax.ShapeDtypeStruct((NZ, 2, 2, CW, LN), BF),
        in_specs=[VM, VM],
        out_specs=VM,
        scratch_shapes=[
            pltpu.VMEM((rows, LN), F32),
            pltpu.VMEM((2, 2 * rows, LN), F32),
            pltpu.VMEM((2, rows, LN), F32),
        ],
        name="corr" if backward else "conv",
    )(m, x)


def middle_kernel(
    conv_ref, gate_ref, w_ref, wp_ref, target_ref,
    dz_ref,
    conv_buf, own, other, w_own, w_other, goal,
    part_a, part_b, relay, landed, second, relay2, landed2,
    cot_a, cot_b, acc, acc_in, dz_buf, dz_in,
    load_sems, send_sems, recv_sems,
):
    z, c = lax.axis_index("ctx"), lax.axis_index("chan")
    core, chip = lax.rem(c, 2), c // 2
    x, y = chip // NR, lax.rem(chip, NR)
    half = w_ref.shape[1] // 2

    def at(xx, yy):
        return {"chan": (lax.rem(xx, NR) * NR + lax.rem(yy, NR)) * 2 + core}

    partner = {"chan": c + 1 - 2 * core}
    loads = [
        pltpu.make_async_copy(src, dst, load_sems.at[i])
        for i, (src, dst) in enumerate(
            (
                (w_ref.at[:, pl.ds(pl.multiple_of(core * half, LN), half)], w_own),
                (wp_ref, w_other),
                (
                    target_ref.at[
                        :, pl.ds(pl.multiple_of(core * half + chip * BL, LN), BL)
                    ],
                    goal,
                ),
            )
        )
    ]
    for load in loads:
        load.start()
    barrier(
        z_peers(z)
        + [partner]
        + [at(x + o, y) for o in range(1, NR)]
        + [at(x, y + o) for o in range(1, NR)]
    )
    cp = Copies(send_sems, recv_sems)

    def exchange(src, dst):
        arrivals = []
        for off in range(1, NZ):
            to = lax.rem(z + off, NZ)
            arrivals.append(cp.start(src.at[to], dst.at[z], {"ctx": to}))
        dst[z] = src[z]
        for copy in arrivals:
            copy.wait_recv()

    exchange(conv_ref, conv_buf)
    for sig in range(2):
        for jj in range(2):
            turned = conv_buf[:, sig, jj].astype(F32).reshape(BL, LN).T
            own[pl.ds(sig * BL + jj * LN, LN)] = (
                gate_ref[pl.ds(jj * LN, LN)] * turned
            ).astype(BF)
    pair = cp.start(own, other, partner)
    loads[0].wait()
    loads[1].wait()
    pair.wait_recv()

    def product(route, dest):
        part = (part_a, part_b)[route]

        def one(e, carry):
            block = dest * NR + e if route == 0 else e * NR + dest
            columns = pl.ds(pl.multiple_of(block * BL, BL), BL)
            rows = pl.ds(route * BL, BL)
            part[dest, e] = (
                jnp.dot(own[rows], w_own[:, columns], preferred_element_type=F32)
                + jnp.dot(other[rows], w_other[:, columns], preferred_element_type=F32)
            ).astype(BF)
            return carry

        lax.fori_loop(0, NR, one, 0)

    def ahead(along_x, o):
        return at(x + o, y) if along_x else at(x, y + o)

    def place(along_x, o):
        return lax.rem((x if along_x else y) + o, NR)

    def scatter(parts, relays, landings, halves, make):
        axes = [make is not None, make is None]
        kept = []
        for r in range(2):
            if make:
                make(r, place(axes[r], 2))
            far = place(axes[r], 2)
            right, left = ahead(axes[r], 1), ahead(axes[r], 3)
            kept.append(
                [
                    cp.start(halves(parts[r], far, 0), relays.at[r, 0], right),
                    cp.start(halves(parts[r], far, 1), relays.at[r, 1], left),
                ]
            )
        for r in range(2):
            if make:
                make(r, place(axes[r], 1))
            kept[r].append(
                cp.start(
                    halves(parts[r], place(axes[r], 1), 1),
                    landings.at[r, 0, 1],
                    ahead(axes[r], 1),
                )
            )
        for r in range(2):
            if make:
                make(r, place(axes[r], 3))
            kept[r].append(
                cp.start(
                    halves(parts[r], place(axes[r], 3), 0),
                    landings.at[r, 1, 0],
                    ahead(axes[r], 3),
                )
            )
        if make:
            for r in range(2):
                make(r, place(axes[r], 0))
        for side in range(2):
            for r in range(2):
                o = (1, 3)[side]
                kept[r][side].wait_recv()
                chunk = halves(parts[r], place(axes[r], o), side)
                chunk[...] = (chunk[...].astype(F32) + relays[r, side].astype(F32)).astype(BF)
                kept[r].append(cp.start(chunk, landings.at[r, side, side], ahead(axes[r], o)))
        for r in range(2):
            for copy in kept[r][2:]:
                copy.wait_recv()

    def halves_of_blocks(ref, q, h):
        return ref.at[q, pl.ds(2 * h, 2)]

    def halves_of_rows(ref, q, h):
        return ref.at[q, pl.ds(h * LN, LN)]

    parts = (part_a, part_b)
    scatter(parts, relay, landed, halves_of_blocks, product)
    for r in range(2):
        me = (x, y)[r]
        for e in range(NR):
            second[r, e] = (
                parts[r][me, e].astype(F32)
                + landed[r, 0, e // 2, e % 2].astype(F32)
                + landed[r, 1, e // 2, e % 2].astype(F32)
            ).astype(BF)
    scatter((second.at[0], second.at[1]), relay2, landed2, halves_of_rows, None)
    sums = []
    for r in range(2):
        me = (y, x)[r]
        sums.append(
            second[r, me].astype(F32)
            + landed2[r, 0].astype(F32).reshape(BL, BL)
            + landed2[r, 1].astype(F32).reshape(BL, BL)
        )

    loads[2].wait()
    scaling = 1.0 / math.sqrt(NZ * BL)
    bent = jnp.tanh(sums[0] - goal[...].astype(F32))
    cot_a[x, y] = (scaling * bent).astype(BF)
    cot_b[y, x] = (scaling * (1.0 - bent * bent) * sums[1]).astype(BF)

    def gather(stage):
        kept = []
        for r in range(2):
            along_x = (r == 0) == (stage == 1)
            right, left = ahead(along_x, 1), ahead(along_x, 3)
            ref, outer = ((cot_a, x), (cot_b, y))[r]

            def half_at(o, h, ref=ref, outer=outer, along_x=along_x):
                slot = place(along_x, o)
                if stage == 0:
                    return ref.at[outer, slot, pl.ds(h * LN, LN)]
                return ref.at[slot, pl.ds(2 * h, 2)]

            kept.append(
                (
                    half_at,
                    right,
                    left,
                    [
                        cp.start(half_at(0, 0), half_at(0, 0), right),
                        cp.start(half_at(0, 1), half_at(0, 1), left),
                        cp.start(half_at(0, 1), half_at(0, 1), right),
                        cp.start(half_at(0, 0), half_at(0, 0), left),
                    ],
                )
            )
        for half_at, right, left, copies in kept:
            copies[0].wait_recv()
            copies.append(cp.start(half_at(3, 0), half_at(3, 0), right))
            copies[1].wait_recv()
            copies.append(cp.start(half_at(1, 1), half_at(1, 1), left))
        for _, _, _, copies in kept:
            for copy in copies[2:]:
                copy.wait_recv()

    gather(0)
    gather(1)

    nt = (((1,), (1,)), ((), ()))
    acc[...] = jnp.zeros_like(acc)

    def back(q, carry):
        for r, cot in enumerate((cot_a, cot_b)):
            for side, w in enumerate((w_own, w_other)):
                total = None
                for e in range(NR):
                    block = q * NR + e if r == 0 else e * NR + q
                    term = lax.dot_general(
                        cot[q, e],
                        w[:, pl.ds(pl.multiple_of(block * BL, BL), BL)],
                        nt,
                        preferred_element_type=F32,
                    )
                    total = term if total is None else total + term
                acc[side, r] += total
        return carry

    lax.fori_loop(0, NR, back, 0)
    swap = cp.start(acc.at[1], acc_in, partner)
    swap.wait_recv()
    for sig in range(2):
        dz = gate_ref[...] * (acc[0, sig] + acc_in[sig])
        for jj in range(2):
            turned = dz[jj * LN : (jj + 1) * LN].T
            dz_buf[:, sig, jj] = turned.reshape(NZ, CW, LN).astype(BF)
    exchange(dz_buf, dz_in)
    dz_ref[...] = dz_in[...]
    cp.drain()


def middle(conv, gate, w, wp, target):
    half = w.shape[1] // 2
    chunk = (NZ, 2, 2, CW, LN)
    n_copies = 2 * (NZ - 1) + 2 + 4 * 12
    return pl.pallas_call(
        middle_kernel,
        out_shape=jax.ShapeDtypeStruct(chunk, BF),
        in_specs=[VM, VM, ANY, ANY, ANY],
        out_specs=VM,
        scratch_shapes=[
            pltpu.VMEM(chunk, BF),
            pltpu.VMEM((2 * BL, BL), BF),
            pltpu.VMEM((2 * BL, BL), BF),
            pltpu.VMEM((BL, half), BF),
            pltpu.VMEM((BL, half), BF),
            pltpu.VMEM((BL, BL), BF),
            pltpu.VMEM((NR, NR, BL, BL), BF),
            pltpu.VMEM((NR, NR, BL, BL), BF),
            pltpu.VMEM((2, 2, 2, BL, BL), BF),
            pltpu.VMEM((2, 2, 2, 2, BL, BL), BF),
            pltpu.VMEM((2, NR, BL, BL), BF),
            pltpu.VMEM((2, 2, LN, BL), BF),
            pltpu.VMEM((2, 2, 2, LN, BL), BF),
            pltpu.VMEM((NR, NR, BL, BL), BF),
            pltpu.VMEM((NR, NR, BL, BL), BF),
            pltpu.VMEM((2, 2, BL, BL), F32),
            pltpu.VMEM((2, BL, BL), F32),
            pltpu.VMEM(chunk, BF),
            pltpu.VMEM(chunk, BF),
            pltpu.SemaphoreType.DMA((3,)),
            pltpu.SemaphoreType.DMA((n_copies,)),
            pltpu.SemaphoreType.DMA((n_copies,)),
        ],
        compiler_params=pltpu.CompilerParams(collective_id=1, has_side_effects=True),
        name="middle",
    )(conv, gate, w, wp, target)


def leave_kernel(src_ref, a_ref, b_ref, in_buf, send_sems, recv_sems):
    z = lax.axis_index("ctx")
    barrier(z_peers(z))
    cp = Copies(send_sems, recv_sems)
    for off in range(1, NZ):
        to = lax.rem(z + off, NZ)
        cp.start(src_ref.at[to], in_buf.at[z], {"ctx": to})
    in_buf[z] = src_ref[z]
    for copy in cp.made:
        copy.wait_recv()
    for sig, ref in enumerate((a_ref, b_ref)):
        for jj in range(2):
            ref[pl.ds(jj * LN, LN)] = (
                in_buf[:, sig, jj].astype(F32).reshape(BL, LN).T.astype(BF)
            )
    cp.drain()


def leave(src):
    return pl.pallas_call(
        leave_kernel,
        out_shape=(jax.ShapeDtypeStruct((BL, BL), BF),) * 2,
        in_specs=[VM],
        out_specs=(VM, VM),
        scratch_shapes=[
            pltpu.VMEM((NZ, 2, 2, CW, LN), BF),
            pltpu.SemaphoreType.DMA((NZ - 1,)),
            pltpu.SemaphoreType.DMA((NZ - 1,)),
        ],
        compiler_params=pltpu.CompilerParams(collective_id=2, has_side_effects=True),
        name="leave",
    )(src)


def on_device(query_rows, key_rows, value_rows, short_taps, long_filter, direction, w_out, target):
    taps = short_taps.reshape(9, BL)
    gate, got, w_other = enter(
        query_rows, key_rows, value_rows, taps, long_filter, direction, w_out
    )
    conv = convolve(False, 2, 0, got, got)
    dz = middle(conv, gate, w_out, w_other, target)
    grad, hvp = leave(convolve(True, 2, 0, got, dz))
    return grad.astype(F32), hvp.astype(F32)


def solution(mesh):
    in_specs = (
        P("ctx", "chan"),
        P("ctx", "chan"),
        P("ctx", "chan"),
        P(None, None, "chan"),
        P("ctx", "chan"),
        P("ctx", "chan"),
        P("chan", None),
        P("ctx", None),
    )
    out_specs = (P("ctx", "chan"), P("ctx", "chan"))
    return jax.shard_map(
        on_device, mesh=mesh, in_specs=in_specs, out_specs=out_specs, check_vma=False
    )
```

```python
import math

import jax
import jax.numpy as jnp
from jax import lax
from jax.experimental import pallas as pl
from jax.experimental.pallas import tpu as pltpu
from jax.sharding import PartitionSpec as P

MESH = pl.DeviceIdType.MESH
BF = jnp.bfloat16
F32 = jnp.float32
VM = pl.BlockSpec(memory_space=pltpu.VMEM)
ANY = pl.BlockSpec(memory_space=pl.ANY)
NZ = 8
NR = 4
BL = 256
LN = 128
NP = 2
CW = BL // NZ
NG = 2
GW = CW // NG
NB = 2 * NZ
N_COPIES = 4 + 2 * 7 + NG * NP * 7 + 2 * NP + NP * 48 + NP * 7 + NG * 7


class Copies:
    def __init__(self, send_sems, recv_sems):
        self.send_sems, self.recv_sems, self.made = send_sems, recv_sems, []

    def start(self, src, dst, device):
        slot = len(self.made)
        copy = pltpu.make_async_remote_copy(
            src_ref=src,
            dst_ref=dst,
            send_sem=self.send_sems.at[slot],
            recv_sem=self.recv_sems.at[slot],
            device_id=device,
            device_id_type=MESH,
        )
        copy.start()
        self.made.append(copy)
        return copy

    def drain(self):
        assert len(self.made) == N_COPIES
        for copy in self.made:
            copy.wait_send()


def arrived(copies):
    for copy in copies:
        copy.wait_recv()


def toeplitz(m_buf, channel):
    row = lax.broadcasted_iota(jnp.int32, (LN, LN), 0)
    lane = lax.broadcasted_iota(jnp.int32, (LN, LN), 1)
    keep = lane >= row
    before = jnp.zeros((LN, LN), F32)
    pieces = []
    for piece in range(NB):
        line = m_buf[pl.ds(piece * CW + channel, 1)]
        turned = pltpu.roll(
            jnp.broadcast_to(line, (LN, LN)), 0, 1, stride=1, stride_axis=0
        )
        pieces.append(jnp.where(keep, turned, before).astype(BF))
        before = turned
    return pieces


def kernel(
    q_ref, k_ref, v_ref, taps_ref, h_ref, d_ref, w_ref, target_ref,
    res_ref,
    halo, ext, gate_t, hdm_out, hdm_in, m_buf, x_buf, y_buf, u_buf,
    conv_out, conv_in, own, other, w_own, w_other, goal,
    part_a, part_b, relay, landed, second, relay2, landed2,
    cot_a, cot_b, acc, acc_in, dz_out, dz_in, res_out, res_in,
    load_sems, send_sems, recv_sems,
):
    z, c = lax.axis_index("ctx"), lax.axis_index("chan")
    core, chip = lax.rem(c, 2), c // 2
    x, y = chip // NR, lax.rem(chip, NR)
    half = w_ref.shape[1] // 2
    cp = Copies(send_sems, recv_sems)

    def at(xx, yy):
        return {"chan": (lax.rem(xx, NR) * NR + lax.rem(yy, NR)) * 2 + core}

    def ahead(along_x, o):
        return at(x + o, y) if along_x else at(x, y + o)

    def place(along_x, o):
        return lax.rem((x if along_x else y) + o, NR)

    partner = {"chan": c + 1 - 2 * core}
    peers = [{"ctx": lax.rem(z + off, NZ)} for off in range(1, NZ)]
    everyone = peers + [partner]
    everyone += [at(x + o, y) for o in (1, 3)] + [at(x, y + o) for o in (1, 3)]
    gate_sem = pltpu.get_barrier_semaphore()
    for device in everyone:
        pl.semaphore_signal(gate_sem, inc=1, device_id=device, device_id_type=MESH)

    loads = [
        pltpu.make_async_copy(src, dst, load_sems.at[i])
        for i, (src, dst) in enumerate(
            (
                (w_ref.at[:, pl.ds(pl.multiple_of(core * half, LN), half)], w_own),
                (
                    target_ref.at[
                        :, pl.ds(pl.multiple_of(core * half + chip * BL, LN), BL)
                    ],
                    goal,
                ),
            )
        )
    ]
    for load in loads:
        load.start()

    def put(value, which):
        for jj in range(2):
            turned = value[jj * LN : (jj + 1) * LN].T
            hdm_out[:, which, jj] = turned.reshape(NZ, CW, LN).astype(BF)

    put(h_ref[...].astype(F32), 0)
    put(d_ref[...].astype(F32), 1)
    pl.semaphore_wait(gate_sem, len(everyone))

    halos = [
        cp.start(ref.at[pl.ds(BL - 16, 16)], halo.at[i], peers[0])
        for i, ref in enumerate((k_ref, v_ref, q_ref))
    ]
    inside = (z > 0).astype(F32)

    def short(i, ref, base):
        halos[i].wait_recv()
        ext[i, pl.ds(0, 16)] = halo[i].astype(F32) * inside
        ext[i, pl.ds(16, BL)] = ref[...].astype(F32)
        return (
            taps_ref[base, pl.ds(0, 1)] * ext[i, pl.ds(16, BL)]
            + taps_ref[base, pl.ds(1, 1)] * ext[i, pl.ds(15, BL)]
            + taps_ref[base, pl.ds(2, 1)] * ext[i, pl.ds(14, BL)]
        )

    def exchange(src_of, dst_of):
        return [
            cp.start(src_of(lax.rem(z + off, NZ)), dst_of(z), peers[off - 1])
            for off in range(1, NZ)
        ]

    put(short(0, k_ref, 1) * short(1, v_ref, 2), 2)
    m_copies = exchange(lambda to: hdm_out.at[to, 2], lambda me: hdm_in.at[me, 2])
    hd_copies = exchange(
        lambda to: hdm_out.at[to, pl.ds(0, 2)], lambda me: hdm_in.at[me, pl.ds(0, 2)]
    )
    w_copy = cp.start(
        w_ref.at[:, pl.ds(pl.multiple_of((1 - core) * half, LN), half)], w_other, partner
    )
    hdm_in[z] = hdm_out[z]
    gate_t[...] = short(2, q_ref, 0).T
    rows = NB * CW
    x_buf[:, pl.ds(0, rows)] = jnp.zeros((2, rows, LN), F32)
    arrived(m_copies)
    for src in range(NZ):
        for jj in range(2):
            m_buf[pl.ds((2 * src + jj) * CW, CW)] = hdm_in[src, 2, jj].astype(F32)

    def build(channel, carry):
        u_buf[channel] = jnp.concatenate(toeplitz(m_buf, channel), axis=1)
        return carry

    lax.fori_loop(0, CW, build, 0)

    def load_x(value_of, first):
        for sig in range(2):
            for src in range(NZ):
                for jj in range(2):
                    x_buf[sig, pl.ds(first + (2 * src + jj) * CW, CW)] = value_of(
                        src, jj, sig
                    ).astype(F32)

    def lines_of(channel, first):
        return jnp.concatenate(
            [
                jnp.concatenate(
                    [x_buf[sig, pl.ds(first(k) + channel, NB, stride=CW)] for sig in range(2)],
                    axis=0,
                ).astype(BF)
                for k in range(NB)
            ],
            axis=1,
        )

    def keep_y(channel, value):
        for sig in range(2):
            y_buf[sig, pl.ds(channel, NB, stride=CW)] = value[sig * NB : (sig + 1) * NB]

    def conv(channel, carry):
        left = lines_of(channel, lambda k: (NB - k) * CW)
        pieces = [u_buf[channel, :, pl.ds(LN * k, LN)] for k in range(NB)]
        keep_y(
            channel,
            jnp.dot(left, jnp.concatenate(pieces, axis=0), preferred_element_type=F32),
        )
        return carry

    def corr(channel, carry):
        left = lines_of(channel, lambda k: k * CW)
        keep_y(
            channel,
            lax.dot_general(
                left, u_buf[channel], (((1,), (1,)), ((), ())), preferred_element_type=F32
            ),
        )
        return carry

    arrived(hd_copies)
    load_x(lambda src, jj, sig: hdm_in[src, sig, jj], rows)
    conv_copies = [[] for _ in range(NP)]
    for g in range(NG):
        lax.fori_loop(g * GW, (g + 1) * GW, conv, 0)
        for jj in range(NP):
            for dest in range(NZ):
                for sig in range(2):
                    conv_out[dest, g, jj, sig] = y_buf[
                        sig, pl.ds((2 * dest + jj) * CW + g * GW, GW)
                    ].astype(BF)
        for jj in range(NP):
            conv_copies[jj] += exchange(
                lambda to, g=g, jj=jj: conv_out.at[to, g, jj],
                lambda me, g=g, jj=jj: conv_in.at[me, g, jj],
            )
    conv_in[z] = conv_out[z]

    pairs = []
    for t in range(NP):
        arrived(conv_copies[t])
        for sig in range(2):
            gated = conv_in[:, :, t, sig].astype(F32).reshape(BL, LN) * gate_t[:, t * LN : (t + 1) * LN]
            own[t, pl.ds(sig * LN, LN)] = gated.T.astype(BF)
        pairs.append(cp.start(own.at[t], other.at[t], partner))
    loads[0].wait()
    w_copy.wait_recv()
    parts = (part_a, part_b)
    crossing = [(part_a, cot_a, True), (part_b, cot_b, False)]

    def product(t, r, dest):
        part = parts[r]
        line = pl.ds(r * LN, LN)

        def one(e, carry):
            block = dest * NR + e if r == 0 else e * NR + dest
            columns = pl.ds(pl.multiple_of(block * BL, BL), BL)
            part[t, dest, e] = (
                jnp.dot(own[t, line], w_own[:, columns], preferred_element_type=F32)
                + jnp.dot(other[t, line], w_other[:, columns], preferred_element_type=F32)
            ).astype(BF)
            return carry

        lax.fori_loop(0, NR, one, 0)

    def products(t, o):
        for r in range(2):
            product(t, r, place(r == 0, o))

    class Scatter:
        def __init__(self, halves, relays, landings, first):
            self.halves, self.relays, self.landings = halves, relays, landings
            self.axes = [first, not first]
            self.far, self.rest = [[], []], [[], []]

        def send_far(self, r):
            a = self.axes[r]
            for side in range(2):
                self.far[r].append(
                    cp.start(
                        self.halves(r, place(a, 2), side),
                        self.relays.at[r, side],
                        ahead(a, (1, 3)[side]),
                    )
                )

        def send_near(self, r, side):
            a, o = self.axes[r], (1, 3)[side]
            self.rest[r].append(
                cp.start(
                    self.halves(r, place(a, o), 1 - side),
                    self.landings.at[r, side, 1 - side],
                    ahead(a, o),
                )
            )

        def pass_on(self):
            for side in range(2):
                for r in range(2):
                    a, o = self.axes[r], (1, 3)[side]
                    self.far[r][side].wait_recv()
                    chunk = self.halves(r, place(a, o), side)
                    chunk[...] = (
                        chunk[...].astype(F32) + self.relays[r, side].astype(F32)
                    ).astype(BF)
                    self.rest[r].append(
                        cp.start(chunk, self.landings.at[r, side, side], ahead(a, o))
                    )

        def wait(self):
            for r in range(2):
                arrived(self.rest[r])

        def start(self):
            for r in range(2):
                self.send_far(r)
            for r in range(2):
                for side in range(2):
                    self.send_near(r, side)

    wide = [
        Scatter(
            lambda r, q, h, t=t: parts[r].at[t, q, pl.ds(2 * h, 2)],
            relay.at[t],
            landed.at[t],
            True,
        )
        for t in range(NP)
    ]
    narrow = [
        Scatter(
            lambda r, q, h, t=t: second.at[t, r, q, pl.ds(h * LN // 2, LN // 2)],
            relay2.at[t],
            landed2.at[t],
            False,
        )
        for t in range(NP)
    ]

    def finish_wide(t):
        wide[t].wait()
        for r in range(2):
            me = (x, y)[r]
            for e in range(NR):
                second[t, r, e] = (
                    parts[r][t, me, e].astype(F32)
                    + landed[t, r, 0, e // 2, e % 2].astype(F32)
                    + landed[t, r, 1, e // 2, e % 2].astype(F32)
                ).astype(BF)
        narrow[t].start()

    class Gather:
        def __init__(self, t, stage):
            self.t, self.stage, self.kept = t, stage, [[], []]

        def half_at(self, r, o, h):
            slot = place((r == 0) == (self.stage == 1), o)
            ref = (cot_a, cot_b)[r]
            if self.stage == 0:
                return ref.at[self.t, (x, y)[r], slot, pl.ds(h * LN, LN)]
            return ref.at[self.t, slot, pl.ds(2 * h, 2)]

        def send(self, r, o, h, side):
            along_x = (r == 0) == (self.stage == 1)
            ref = self.half_at(r, o, h)
            self.kept[r].append(cp.start(ref, ref, ahead(along_x, (1, 3)[side])))

        def start(self):
            for r in range(2):
                self.send(r, 0, 0, 0)
                self.send(r, 0, 1, 1)
            for r in range(2):
                self.send(r, 0, 1, 0)
                self.send(r, 0, 0, 1)

        def pass_on(self):
            for r in range(2):
                self.kept[r][0].wait_recv()
                self.send(r, 3, 0, 0)
                self.kept[r][1].wait_recv()
                self.send(r, 1, 1, 1)

        def wait(self):
            for r in range(2):
                arrived(self.kept[r][2:])

    gathers = [[Gather(t, stage) for stage in range(2)] for t in range(NP)]
    scaling = 1.0 / math.sqrt(NZ * BL)

    def cotangents(t):
        narrow[t].wait()
        sums = [
            second[t, r, (y, x)[r]].astype(F32)
            + landed2[t, r, 0].astype(F32).reshape(LN, BL)
            + landed2[t, r, 1].astype(F32).reshape(LN, BL)
            for r in range(2)
        ]
        bent = jnp.tanh(sums[0] - goal[pl.ds(t * LN, LN)].astype(F32))
        cot_a[t, x, y] = (scaling * bent).T.astype(BF)
        cot_b[t, y, x] = (scaling * (1.0 - bent * bent) * sums[1]).T.astype(BF)
        gathers[t][0].start()

    def widen(t):
        gathers[t][0].wait()
        gathers[t][1].start()

    swaps = [None] * NP

    def back(t):
        gathers[t][1].wait()
        acc[t] = jnp.zeros_like(acc[t])

        def one(q, carry):
            for side, w in enumerate((w_own, w_other)):
                total = None
                for e in range(NR):
                    right = jnp.concatenate([cot_a[t, q, e], cot_b[t, e, q]], axis=1)
                    columns = pl.ds(pl.multiple_of((q * NR + e) * BL, BL), BL)
                    term = jnp.dot(w[:, columns], right, preferred_element_type=F32)
                    total = term if total is None else total + term
                acc[t, side] += total
            return carry

        lax.fori_loop(0, NR, one, 0)
        swaps[t] = cp.start(acc.at[t, 1], acc_in.at[t], partner)

    dz_copies = []

    def send_dz(t):
        swaps[t].wait_recv()
        for sig in range(2):
            lanes = slice(sig * LN, (sig + 1) * LN)
            dz = gate_t[:, t * LN : (t + 1) * LN] * (acc[t, 0, :, lanes] + acc_in[t, :, lanes])
            dz_out[:, t, sig] = dz.reshape(NZ, CW, LN).astype(BF)
        dz_copies.extend(exchange(lambda to: dz_out.at[to, t], lambda me: dz_in.at[me, t]))

    pairs[0].wait_recv()
    products(0, 2)
    for r in range(2):
        wide[0].send_far(r)
    products(0, 1)
    for r in range(2):
        wide[0].send_near(r, 0)
    products(0, 3)
    for r in range(2):
        wide[0].send_near(r, 1)
    products(0, 0)
    pairs[1].wait_recv()
    products(1, 2)
    wide[0].pass_on()
    for r in range(2):
        wide[1].send_far(r)
    products(1, 1)
    products(1, 3)
    for r in range(2):
        for side in range(2):
            wide[1].send_near(r, side)
    products(1, 0)
    finish_wide(0)
    wide[1].pass_on()
    narrow[0].pass_on()
    loads[1].wait()
    cotangents(0)
    finish_wide(1)
    gathers[0][0].pass_on()
    narrow[1].pass_on()
    widen(0)
    cotangents(1)
    gathers[1][0].pass_on()
    gathers[0][1].pass_on()
    widen(1)
    back(0)
    gathers[1][1].pass_on()
    send_dz(0)
    back(1)
    x_buf[:, pl.ds(rows, rows)] = jnp.zeros((2, rows, LN), F32)
    send_dz(1)
    dz_in[z] = dz_out[z]
    arrived(dz_copies)

    load_x(lambda src, jj, sig: dz_in[src, jj, sig], 0)
    res_copies = []
    for g in range(NG):
        lax.fori_loop(g * GW, (g + 1) * GW, corr, 0)
        for dest in range(NZ):
            for jj in range(2):
                for sig in range(2):
                    res_out[dest, g, jj, sig] = y_buf[
                        sig, pl.ds((2 * dest + jj) * CW + g * GW, GW)
                    ].astype(BF)
        res_copies += exchange(
            lambda to, g=g: res_out.at[to, g], lambda me, g=g: res_in.at[me, g]
        )
    res_in[z] = res_out[z]
    arrived(res_copies)
    res_ref[...] = res_in[...]
    cp.drain()


def products_of_a_step(q, k, v, taps, h, d, w, target):
    half = w.shape[1] // 2
    rows = NB * CW
    hdm = (NZ, 3, 2, CW, LN)
    groups = (NZ, NG, NP, 2, GW, LN)
    plain = (NZ, NP, 2, CW, LN)
    return pl.pallas_call(
        kernel,
        out_shape=jax.ShapeDtypeStruct(groups, BF),
        in_specs=[VM] * 6 + [ANY, ANY],
        out_specs=VM,
        scratch_shapes=[
            pltpu.VMEM((3, 16, BL), BF),
            pltpu.VMEM((3, BL + 16, BL), F32),
            pltpu.VMEM((BL, BL), F32),
            pltpu.VMEM(hdm, BF),
            pltpu.VMEM(hdm, BF),
            pltpu.VMEM((rows, LN), F32),
            pltpu.VMEM((2, 2 * rows, LN), F32),
            pltpu.VMEM((2, rows, LN), F32),
            pltpu.VMEM((CW, LN, NB * LN), BF),
            pltpu.VMEM(groups, BF),
            pltpu.VMEM(groups, BF),
            pltpu.VMEM((NP, BL, BL), BF),
            pltpu.VMEM((NP, BL, BL), BF),
            pltpu.VMEM((BL, half), BF),
            pltpu.VMEM((BL, half), BF),
            pltpu.VMEM((BL, BL), BF),
            pltpu.VMEM((NP, NR, NR, LN, BL), BF),
            pltpu.VMEM((NP, NR, NR, LN, BL), BF),
            pltpu.VMEM((NP, 2, 2, 2, LN, BL), BF),
            pltpu.VMEM((NP, 2, 2, 2, 2, LN, BL), BF),
            pltpu.VMEM((NP, 2, NR, LN, BL), BF),
            pltpu.VMEM((NP, 2, 2, LN // 2, BL), BF),
            pltpu.VMEM((NP, 2, 2, 2, LN // 2, BL), BF),
            pltpu.VMEM((NP, NR, NR, BL, LN), BF),
            pltpu.VMEM((NP, NR, NR, BL, LN), BF),
            pltpu.VMEM((NP, 2, BL, BL), F32),
            pltpu.VMEM((NP, BL, BL), F32),
            pltpu.VMEM(plain, BF),
            pltpu.VMEM(plain, BF),
            pltpu.VMEM(groups, BF),
            pltpu.VMEM(groups, BF),
            pltpu.SemaphoreType.DMA((2,)),
            pltpu.SemaphoreType.DMA((N_COPIES,)),
            pltpu.SemaphoreType.DMA((N_COPIES,)),
        ],
        compiler_params=pltpu.CompilerParams(
            collective_id=0, has_side_effects=True, vmem_limit_bytes=60 * 2**20
        ),
        name="step",
    )(q, k, v, taps, h, d, w, target)


def unfold_kernel(src_ref, a_ref, b_ref):
    for sig, ref in enumerate((a_ref, b_ref)):
        for jj in range(2):
            ref[pl.ds(jj * LN, LN)] = src_ref[:, :, jj, sig].astype(F32).reshape(BL, LN).T


def unfold(src):
    return pl.pallas_call(
        unfold_kernel,
        out_shape=(jax.ShapeDtypeStruct((BL, BL), F32),) * 2,
        in_specs=[VM],
        out_specs=(VM, VM),
        name="unfold",
    )(src)


def on_device(*args):
    return unfold(products_of_a_step(*args))


def solution(mesh):
    in_specs = (
        P("ctx", "chan"),
        P("ctx", "chan"),
        P("ctx", "chan"),
        P(None, None, "chan"),
        P("ctx", "chan"),
        P("ctx", "chan"),
        P("chan", None),
        P("ctx", None),
    )
    out_specs = (P("ctx", "chan"), P("ctx", "chan"))
    return jax.shard_map(
        on_device, mesh=mesh, in_specs=in_specs, out_specs=out_specs, check_vma=False
    )
```

```python
import math

import jax
import jax.numpy as jnp
from jax import lax
from jax.experimental import pallas as pl
from jax.experimental.pallas import tpu as pltpu
from jax.sharding import PartitionSpec as P

MESH = pl.DeviceIdType.MESH
BF = jnp.bfloat16
F32 = jnp.float32
VM = pl.BlockSpec(memory_space=pltpu.VMEM)
ANY = pl.BlockSpec(memory_space=pl.ANY)
NZ = 8
NR = 4
BL = 256
LN = 128
NP = 2
CW = BL // NZ
NG = 2
GW = CW // NG
NB = 2 * NZ
BU, CU = 1, 8
N_COPIES = 4 + 2 * 7 + NG * NP * 7 + 2 * NP + NP * 48 + NP * 7 + NG * 7


class Copies:
    def __init__(self, send_sems, recv_sems):
        self.send_sems, self.recv_sems, self.made = send_sems, recv_sems, []

    def start(self, src, dst, device):
        slot = len(self.made)
        copy = pltpu.make_async_remote_copy(
            src_ref=src,
            dst_ref=dst,
            send_sem=self.send_sems.at[slot],
            recv_sem=self.recv_sems.at[slot],
            device_id=device,
            device_id_type=MESH,
        )
        copy.start()
        self.made.append(copy)
        return copy

    def drain(self):
        assert len(self.made) == N_COPIES
        for copy in self.made:
            copy.wait_send()


def arrived(copies):
    for copy in copies:
        copy.wait_recv()


def toeplitz(m_buf, channel):
    row = lax.broadcasted_iota(jnp.int32, (LN, LN), 0)
    lane = lax.broadcasted_iota(jnp.int32, (LN, LN), 1)
    keep = lane >= row
    before = jnp.zeros((LN, LN), F32)
    pieces = []
    for piece in range(NB):
        line = m_buf[pl.ds(piece * CW + channel, 1)]
        turned = pltpu.roll(
            jnp.broadcast_to(line, (LN, LN)), 0, 1, stride=1, stride_axis=0
        )
        pieces.append(jnp.where(keep, turned, before).astype(BF))
        before = turned
    return pieces


def kernel(
    q_ref, k_ref, v_ref, taps_ref, h_ref, d_ref, w_ref, target_ref,
    res_ref,
    halo, ext, gate_t, hdm_out, hdm_in, m_buf, x_buf, y_buf, u_buf,
    conv_out, conv_in, own, other, w_own, w_other, goal,
    part_a, part_b, relay, landed, second, relay2, landed2,
    cot_a, cot_b, acc, acc_in, dz_out, dz_in, res_out, res_in,
    load_sems, send_sems, recv_sems,
):
    z, c = lax.axis_index("ctx"), lax.axis_index("chan")
    core, chip = lax.rem(c, 2), c // 2
    x, y = chip // NR, lax.rem(chip, NR)
    half = w_ref.shape[1] // 2
    cp = Copies(send_sems, recv_sems)

    def at(xx, yy):
        return {"chan": (lax.rem(xx, NR) * NR + lax.rem(yy, NR)) * 2 + core}

    def ahead(along_x, o):
        return at(x + o, y) if along_x else at(x, y + o)

    def place(along_x, o):
        return lax.rem((x if along_x else y) + o, NR)

    partner = {"chan": c + 1 - 2 * core}
    peers = [{"ctx": lax.rem(z + off, NZ)} for off in range(1, NZ)]
    everyone = peers + [partner]
    everyone += [at(x + o, y) for o in (1, 3)] + [at(x, y + o) for o in (1, 3)]
    gate_sem = pltpu.get_barrier_semaphore()
    for device in everyone:
        pl.semaphore_signal(gate_sem, inc=1, device_id=device, device_id_type=MESH)

    loads = [
        pltpu.make_async_copy(src, dst, load_sems.at[i])
        for i, (src, dst) in enumerate(
            (
                (w_ref.at[:, pl.ds(pl.multiple_of(core * half, LN), half)], w_own),
                (
                    target_ref.at[
                        :, pl.ds(pl.multiple_of(core * half + chip * BL, LN), BL)
                    ],
                    goal,
                ),
            )
        )
    ]
    for load in loads:
        load.start()

    def put(value, which):
        for jj in range(2):
            turned = value[jj * LN : (jj + 1) * LN].T
            hdm_out[:, which, jj] = turned.reshape(NZ, CW, LN).astype(BF)

    put(h_ref[...].astype(F32), 0)
    put(d_ref[...].astype(F32), 1)
    pl.semaphore_wait(gate_sem, len(everyone))

    halos = [
        cp.start(ref.at[pl.ds(BL - 16, 16)], halo.at[i], peers[0])
        for i, ref in enumerate((k_ref, v_ref, q_ref))
    ]
    inside = (z > 0).astype(F32)

    def short(i, ref, base):
        halos[i].wait_recv()
        ext[i, pl.ds(0, 16)] = halo[i].astype(F32) * inside
        ext[i, pl.ds(16, BL)] = ref[...].astype(F32)
        return (
            taps_ref[base, pl.ds(0, 1)] * ext[i, pl.ds(16, BL)]
            + taps_ref[base, pl.ds(1, 1)] * ext[i, pl.ds(15, BL)]
            + taps_ref[base, pl.ds(2, 1)] * ext[i, pl.ds(14, BL)]
        )

    def exchange(src_of, dst_of):
        return [
            cp.start(src_of(lax.rem(z + off, NZ)), dst_of(z), peers[off - 1])
            for off in range(1, NZ)
        ]

    put(short(0, k_ref, 1) * short(1, v_ref, 2), 2)
    m_copies = exchange(lambda to: hdm_out.at[to, 2], lambda me: hdm_in.at[me, 2])
    hd_copies = exchange(
        lambda to: hdm_out.at[to, pl.ds(0, 2)], lambda me: hdm_in.at[me, pl.ds(0, 2)]
    )
    w_copy = cp.start(
        w_ref.at[:, pl.ds(pl.multiple_of((1 - core) * half, LN), half)], w_other, partner
    )
    hdm_in[z] = hdm_out[z]
    gate_t[...] = short(2, q_ref, 0).T
    rows = NB * CW
    x_buf[:, pl.ds(0, rows)] = jnp.zeros((2, rows, LN), F32)
    arrived(m_copies)
    for src in range(NZ):
        for jj in range(2):
            m_buf[pl.ds((2 * src + jj) * CW, CW)] = hdm_in[src, 2, jj].astype(F32)

    def build(channel, carry):
        u_buf[channel] = jnp.concatenate(toeplitz(m_buf, channel), axis=1)
        return carry

    lax.fori_loop(0, CW, build, 0, unroll=BU)

    def load_x(value_of, first):
        for sig in range(2):
            for src in range(NZ):
                for jj in range(2):
                    x_buf[sig, pl.ds(first + (2 * src + jj) * CW, CW)] = value_of(
                        src, jj, sig
                    ).astype(F32)

    def lines_of(channel, first):
        return jnp.concatenate(
            [
                jnp.concatenate(
                    [x_buf[sig, pl.ds(first(k) + channel, NB, stride=CW)] for sig in range(2)],
                    axis=0,
                ).astype(BF)
                for k in range(NB)
            ],
            axis=1,
        )

    def keep_y(channel, value):
        for sig in range(2):
            y_buf[sig, pl.ds(channel, NB, stride=CW)] = value[sig * NB : (sig + 1) * NB]

    def conv(channel, carry):
        left = lines_of(channel, lambda k: (NB - k) * CW)
        pieces = [u_buf[channel, :, pl.ds(LN * k, LN)] for k in range(NB)]
        keep_y(
            channel,
            jnp.dot(left, jnp.concatenate(pieces, axis=0), preferred_element_type=F32),
        )
        return carry

    def corr(channel, carry):
        left = lines_of(channel, lambda k: k * CW)
        keep_y(
            channel,
            lax.dot_general(
                left, u_buf[channel], (((1,), (1,)), ((), ())), preferred_element_type=F32
            ),
        )
        return carry

    arrived(hd_copies)
    load_x(lambda src, jj, sig: hdm_in[src, sig, jj], rows)
    conv_copies = [[] for _ in range(NP)]
    for g in range(NG):
        lax.fori_loop(g * GW, (g + 1) * GW, conv, 0, unroll=CU)
        for jj in range(NP):
            for dest in range(NZ):
                for sig in range(2):
                    conv_out[dest, g, jj, sig] = y_buf[
                        sig, pl.ds((2 * dest + jj) * CW + g * GW, GW)
                    ].astype(BF)
        for jj in range(NP):
            conv_copies[jj] += exchange(
                lambda to, g=g, jj=jj: conv_out.at[to, g, jj],
                lambda me, g=g, jj=jj: conv_in.at[me, g, jj],
            )
    conv_in[z] = conv_out[z]

    pairs = []
    for t in range(NP):
        arrived(conv_copies[t])
        for sig in range(2):
            gated = conv_in[:, :, t, sig].astype(F32).reshape(BL, LN) * gate_t[:, t * LN : (t + 1) * LN]
            own[t, pl.ds(sig * LN, LN)] = gated.T.astype(BF)
        pairs.append(cp.start(own.at[t], other.at[t], partner))
    loads[0].wait()
    w_copy.wait_recv()
    parts = (part_a, part_b)
    crossing = [(part_a, cot_a, True), (part_b, cot_b, False)]

    def product(t, r, dest):
        part = parts[r]
        line = pl.ds(r * LN, LN)

        def one(e, carry):
            block = dest * NR + e if r == 0 else e * NR + dest
            columns = pl.ds(pl.multiple_of(block * BL, BL), BL)
            part[t, dest, e] = (
                jnp.dot(own[t, line], w_own[:, columns], preferred_element_type=F32)
                + jnp.dot(other[t, line], w_other[:, columns], preferred_element_type=F32)
            ).astype(BF)
            return carry

        lax.fori_loop(0, NR, one, 0)

    def products(t, o):
        for r in range(2):
            product(t, r, place(r == 0, o))

    class Scatter:
        def __init__(self, halves, relays, landings, first):
            self.halves, self.relays, self.landings = halves, relays, landings
            self.axes = [first, not first]
            self.far, self.rest = [[], []], [[], []]

        def send_far(self, r):
            a = self.axes[r]
            for side in range(2):
                self.far[r].append(
                    cp.start(
                        self.halves(r, place(a, 2), side),
                        self.relays.at[r, side],
                        ahead(a, (1, 3)[side]),
                    )
                )

        def send_near(self, r, side):
            a, o = self.axes[r], (1, 3)[side]
            self.rest[r].append(
                cp.start(
                    self.halves(r, place(a, o), 1 - side),
                    self.landings.at[r, side, 1 - side],
                    ahead(a, o),
                )
            )

        def pass_on(self):
            for side in range(2):
                for r in range(2):
                    a, o = self.axes[r], (1, 3)[side]
                    self.far[r][side].wait_recv()
                    chunk = self.halves(r, place(a, o), side)
                    chunk[...] = (
                        chunk[...].astype(F32) + self.relays[r, side].astype(F32)
                    ).astype(BF)
                    self.rest[r].append(
                        cp.start(chunk, self.landings.at[r, side, side], ahead(a, o))
                    )

        def wait(self):
            for r in range(2):
                arrived(self.rest[r])

        def start(self):
            for r in range(2):
                self.send_far(r)
            for r in range(2):
                for side in range(2):
                    self.send_near(r, side)

    wide = [
        Scatter(
            lambda r, q, h, t=t: parts[r].at[t, q, pl.ds(2 * h, 2)],
            relay.at[t],
            landed.at[t],
            True,
        )
        for t in range(NP)
    ]
    narrow = [
        Scatter(
            lambda r, q, h, t=t: second.at[t, r, q, pl.ds(h * LN // 2, LN // 2)],
            relay2.at[t],
            landed2.at[t],
            False,
        )
        for t in range(NP)
    ]

    def finish_wide(t):
        wide[t].wait()
        for r in range(2):
            me = (x, y)[r]
            for e in range(NR):
                second[t, r, e] = (
                    parts[r][t, me, e].astype(F32)
                    + landed[t, r, 0, e // 2, e % 2].astype(F32)
                    + landed[t, r, 1, e // 2, e % 2].astype(F32)
                ).astype(BF)
        narrow[t].start()

    class Gather:
        def __init__(self, t, stage):
            self.t, self.stage, self.kept = t, stage, [[], []]

        def half_at(self, r, o, h):
            slot = place((r == 0) == (self.stage == 1), o)
            ref = (cot_a, cot_b)[r]
            if self.stage == 0:
                return ref.at[self.t, (x, y)[r], slot, pl.ds(h * LN, LN)]
            return ref.at[self.t, slot, pl.ds(2 * h, 2)]

        def send(self, r, o, h, side):
            along_x = (r == 0) == (self.stage == 1)
            ref = self.half_at(r, o, h)
            self.kept[r].append(cp.start(ref, ref, ahead(along_x, (1, 3)[side])))

        def start(self):
            for r in range(2):
                self.send(r, 0, 0, 0)
                self.send(r, 0, 1, 1)
            for r in range(2):
                self.send(r, 0, 1, 0)
                self.send(r, 0, 0, 1)

        def pass_on(self):
            for r in range(2):
                self.kept[r][0].wait_recv()
                self.send(r, 3, 0, 0)
                self.kept[r][1].wait_recv()
                self.send(r, 1, 1, 1)

        def wait(self):
            for r in range(2):
                arrived(self.kept[r][2:])

    gathers = [[Gather(t, stage) for stage in range(2)] for t in range(NP)]
    scaling = 1.0 / math.sqrt(NZ * BL)

    def cotangents(t):
        narrow[t].wait()
        sums = [
            second[t, r, (y, x)[r]].astype(F32)
            + landed2[t, r, 0].astype(F32).reshape(LN, BL)
            + landed2[t, r, 1].astype(F32).reshape(LN, BL)
            for r in range(2)
        ]
        bent = jnp.tanh(sums[0] - goal[pl.ds(t * LN, LN)].astype(F32))
        cot_a[t, x, y] = (scaling * bent).T.astype(BF)
        cot_b[t, y, x] = (scaling * (1.0 - bent * bent) * sums[1]).T.astype(BF)
        gathers[t][0].start()

    def widen(t):
        gathers[t][0].wait()
        gathers[t][1].start()

    swaps = [None] * NP

    def back(t):
        gathers[t][1].wait()
        acc[t] = jnp.zeros_like(acc[t])

        def one(q, carry):
            for side, w in enumerate((w_own, w_other)):
                total = None
                for e in range(NR):
                    right = jnp.concatenate([cot_a[t, q, e], cot_b[t, e, q]], axis=1)
                    columns = pl.ds(pl.multiple_of((q * NR + e) * BL, BL), BL)
                    term = jnp.dot(w[:, columns], right, preferred_element_type=F32)
                    total = term if total is None else total + term
                acc[t, side] += total
            return carry

        lax.fori_loop(0, NR, one, 0)
        swaps[t] = cp.start(acc.at[t, 1], acc_in.at[t], partner)

    dz_copies = []

    def send_dz(t):
        swaps[t].wait_recv()
        for sig in range(2):
            lanes = slice(sig * LN, (sig + 1) * LN)
            dz = gate_t[:, t * LN : (t + 1) * LN] * (acc[t, 0, :, lanes] + acc_in[t, :, lanes])
            dz_out[:, t, sig] = dz.reshape(NZ, CW, LN).astype(BF)
        dz_copies.extend(exchange(lambda to: dz_out.at[to, t], lambda me: dz_in.at[me, t]))

    pairs[0].wait_recv()
    products(0, 2)
    for r in range(2):
        wide[0].send_far(r)
    products(0, 1)
    for r in range(2):
        wide[0].send_near(r, 0)
    products(0, 3)
    for r in range(2):
        wide[0].send_near(r, 1)
    products(0, 0)
    pairs[1].wait_recv()
    products(1, 2)
    wide[0].pass_on()
    for r in range(2):
        wide[1].send_far(r)
    products(1, 1)
    products(1, 3)
    for r in range(2):
        for side in range(2):
            wide[1].send_near(r, side)
    products(1, 0)
    finish_wide(0)
    wide[1].pass_on()
    narrow[0].pass_on()
    loads[1].wait()
    cotangents(0)
    finish_wide(1)
    gathers[0][0].pass_on()
    narrow[1].pass_on()
    widen(0)
    cotangents(1)
    gathers[1][0].pass_on()
    gathers[0][1].pass_on()
    widen(1)
    back(0)
    gathers[1][1].pass_on()
    send_dz(0)
    back(1)
    x_buf[:, pl.ds(rows, rows)] = jnp.zeros((2, rows, LN), F32)
    send_dz(1)
    dz_in[z] = dz_out[z]
    arrived(dz_copies)

    load_x(lambda src, jj, sig: dz_in[src, jj, sig], 0)
    res_copies = []
    for g in range(NG):
        lax.fori_loop(g * GW, (g + 1) * GW, corr, 0, unroll=CU)
        for dest in range(NZ):
            for jj in range(2):
                for sig in range(2):
                    res_out[dest, g, jj, sig] = y_buf[
                        sig, pl.ds((2 * dest + jj) * CW + g * GW, GW)
                    ].astype(BF)
        res_copies += exchange(
            lambda to, g=g: res_out.at[to, g], lambda me, g=g: res_in.at[me, g]
        )
    res_in[z] = res_out[z]
    arrived(res_copies)
    res_ref[...] = res_in[...]
    cp.drain()


def products_of_a_step(q, k, v, taps, h, d, w, target):
    half = w.shape[1] // 2
    rows = NB * CW
    hdm = (NZ, 3, 2, CW, LN)
    groups = (NZ, NG, NP, 2, GW, LN)
    plain = (NZ, NP, 2, CW, LN)
    return pl.pallas_call(
        kernel,
        out_shape=jax.ShapeDtypeStruct(groups, BF),
        in_specs=[VM] * 6 + [ANY, ANY],
        out_specs=VM,
        scratch_shapes=[
            pltpu.VMEM((3, 16, BL), BF),
            pltpu.VMEM((3, BL + 16, BL), F32),
            pltpu.VMEM((BL, BL), F32),
            pltpu.VMEM(hdm, BF),
            pltpu.VMEM(hdm, BF),
            pltpu.VMEM((rows, LN), F32),
            pltpu.VMEM((2, 2 * rows, LN), F32),
            pltpu.VMEM((2, rows, LN), F32),
            pltpu.VMEM((CW, LN, NB * LN), BF),
            pltpu.VMEM(groups, BF),
            pltpu.VMEM(groups, BF),
            pltpu.VMEM((NP, BL, BL), BF),
            pltpu.VMEM((NP, BL, BL), BF),
            pltpu.VMEM((BL, half), BF),
            pltpu.VMEM((BL, half), BF),
            pltpu.VMEM((BL, BL), BF),
            pltpu.VMEM((NP, NR, NR, LN, BL), BF),
            pltpu.VMEM((NP, NR, NR, LN, BL), BF),
            pltpu.VMEM((NP, 2, 2, 2, LN, BL), BF),
            pltpu.VMEM((NP, 2, 2, 2, 2, LN, BL), BF),
            pltpu.VMEM((NP, 2, NR, LN, BL), BF),
            pltpu.VMEM((NP, 2, 2, LN // 2, BL), BF),
            pltpu.VMEM((NP, 2, 2, 2, LN // 2, BL), BF),
            pltpu.VMEM((NP, NR, NR, BL, LN), BF),
            pltpu.VMEM((NP, NR, NR, BL, LN), BF),
            pltpu.VMEM((NP, 2, BL, BL), F32),
            pltpu.VMEM((NP, BL, BL), F32),
            pltpu.VMEM(plain, BF),
            pltpu.VMEM(plain, BF),
            pltpu.VMEM(groups, BF),
            pltpu.VMEM(groups, BF),
            pltpu.SemaphoreType.DMA((2,)),
            pltpu.SemaphoreType.DMA((N_COPIES,)),
            pltpu.SemaphoreType.DMA((N_COPIES,)),
        ],
        compiler_params=pltpu.CompilerParams(
            collective_id=0, has_side_effects=True, vmem_limit_bytes=60 * 2**20
        ),
        name="step",
    )(q, k, v, taps, h, d, w, target)


def unfold_kernel(src_ref, a_ref, b_ref):
    for sig, ref in enumerate((a_ref, b_ref)):
        for jj in range(2):
            ref[pl.ds(jj * LN, LN)] = src_ref[:, :, jj, sig].astype(F32).reshape(BL, LN).T


def unfold(src):
    return pl.pallas_call(
        unfold_kernel,
        out_shape=(jax.ShapeDtypeStruct((BL, BL), F32),) * 2,
        in_specs=[VM],
        out_specs=(VM, VM),
        name="unfold",
    )(src)


def on_device(*args):
    return unfold(products_of_a_step(*args))


def solution(mesh):
    in_specs = (
        P("ctx", "chan"),
        P("ctx", "chan"),
        P("ctx", "chan"),
        P(None, None, "chan"),
        P("ctx", "chan"),
        P("ctx", "chan"),
        P("chan", None),
        P("ctx", None),
    )
    out_specs = (P("ctx", "chan"), P("ctx", "chan"))
    return jax.shard_map(
        on_device, mesh=mesh, in_specs=in_specs, out_specs=out_specs, check_vma=False
    )
```

```python
import math

import jax
import jax.numpy as jnp
from jax import lax
from jax.experimental import pallas as pl
from jax.experimental.pallas import tpu as pltpu
from jax.sharding import PartitionSpec as P

MESH = pl.DeviceIdType.MESH
BF = jnp.bfloat16
F32 = jnp.float32
VM = pl.BlockSpec(memory_space=pltpu.VMEM)
ANY = pl.BlockSpec(memory_space=pl.ANY)
NZ = 8
NR = 4
BL = 256
LN = 128
NP = 2
CW = BL // NZ
NG = 2
GW = CW // NG
NB = 2 * NZ
BU, CU = 1, 8
N_COPIES = 4 + 2 * 7 + NG * NP * 7 + 2 * NP + NP * 48 + NP * 7 + NG * 7


class Copies:
    def __init__(self, send_sems, recv_sems):
        self.send_sems, self.recv_sems, self.made = send_sems, recv_sems, []

    def start(self, src, dst, device):
        slot = len(self.made)
        copy = pltpu.make_async_remote_copy(
            src_ref=src,
            dst_ref=dst,
            send_sem=self.send_sems.at[slot],
            recv_sem=self.recv_sems.at[slot],
            device_id=device,
            device_id_type=MESH,
        )
        copy.start()
        self.made.append(copy)
        return copy

    def drain(self):
        assert len(self.made) == N_COPIES
        for copy in self.made:
            copy.wait_send()


def arrived(copies):
    for copy in copies:
        copy.wait_recv()


def toeplitz(m_buf, channel):
    row = lax.broadcasted_iota(jnp.int32, (LN, LN), 0)
    lane = lax.broadcasted_iota(jnp.int32, (LN, LN), 1)
    keep = lane >= row
    before = jnp.zeros((LN, LN), F32)
    pieces = []
    for piece in range(NB):
        line = m_buf[pl.ds(piece * CW + channel, 1)]
        turned = pltpu.roll(
            jnp.broadcast_to(line, (LN, LN)), 0, 1, stride=1, stride_axis=0
        )
        pieces.append(jnp.where(keep, turned, before).astype(BF))
        before = turned
    return pieces


def kernel(
    q_ref, k_ref, v_ref, taps_ref, h_ref, d_ref, w_ref, target_ref,
    res_ref,
    halo, ext, gate_t, hdm_out, hdm_in, m_buf, x_buf, y_buf, u_buf,
    conv_out, conv_in, own, other, w_own, w_other, goal,
    part_a, part_b, relay, landed, second, relay2, landed2,
    cot_a, cot_b, acc, acc_in, dz_out, dz_in, res_out, res_in,
    load_sems, send_sems, recv_sems,
):
    z, c = lax.axis_index("ctx"), lax.axis_index("chan")
    core, chip = lax.rem(c, 2), c // 2
    x, y = chip // NR, lax.rem(chip, NR)
    half = w_ref.shape[1] // 2
    cp = Copies(send_sems, recv_sems)

    def at(xx, yy):
        return {"chan": (lax.rem(xx, NR) * NR + lax.rem(yy, NR)) * 2 + core}

    def ahead(along_x, o):
        return at(x + o, y) if along_x else at(x, y + o)

    def place(along_x, o):
        return lax.rem((x if along_x else y) + o, NR)

    partner = {"chan": c + 1 - 2 * core}
    peers = [{"ctx": lax.rem(z + off, NZ)} for off in range(1, NZ)]
    everyone = peers + [partner]
    everyone += [at(x + o, y) for o in (1, 3)] + [at(x, y + o) for o in (1, 3)]
    gate_sem = pltpu.get_barrier_semaphore()
    for device in everyone:
        pl.semaphore_signal(gate_sem, inc=1, device_id=device, device_id_type=MESH)

    loads = [
        pltpu.make_async_copy(src, dst, load_sems.at[i])
        for i, (src, dst) in enumerate(
            (
                (w_ref.at[:, pl.ds(pl.multiple_of(core * half, LN), half)], w_own),
                (
                    target_ref.at[
                        :, pl.ds(pl.multiple_of(core * half + chip * BL, LN), BL)
                    ],
                    goal,
                ),
            )
        )
    ]
    for load in loads:
        load.start()

    def put(value, which):
        for jj in range(2):
            turned = value[jj * LN : (jj + 1) * LN].T
            hdm_out[:, which, jj] = turned.reshape(NZ, CW, LN).astype(BF)

    put(h_ref[...].astype(F32), 0)
    put(d_ref[...].astype(F32), 1)
    pl.semaphore_wait(gate_sem, len(everyone))

    halos = [
        cp.start(ref.at[pl.ds(BL - 16, 16)], halo.at[i], peers[0])
        for i, ref in enumerate((k_ref, v_ref, q_ref))
    ]
    inside = (z > 0).astype(F32)

    def short(i, ref, base):
        halos[i].wait_recv()
        ext[i, pl.ds(0, 16)] = halo[i].astype(F32) * inside
        ext[i, pl.ds(16, BL)] = ref[...].astype(F32)
        return (
            taps_ref[base, pl.ds(0, 1)] * ext[i, pl.ds(16, BL)]
            + taps_ref[base, pl.ds(1, 1)] * ext[i, pl.ds(15, BL)]
            + taps_ref[base, pl.ds(2, 1)] * ext[i, pl.ds(14, BL)]
        )

    def exchange(src_of, dst_of):
        return [
            cp.start(src_of(lax.rem(z + off, NZ)), dst_of(z), peers[off - 1])
            for off in range(1, NZ)
        ]

    put(short(0, k_ref, 1) * short(1, v_ref, 2), 2)
    m_copies = exchange(lambda to: hdm_out.at[to, 2], lambda me: hdm_in.at[me, 2])
    hd_copies = exchange(
        lambda to: hdm_out.at[to, pl.ds(0, 2)], lambda me: hdm_in.at[me, pl.ds(0, 2)]
    )
    w_copy = cp.start(
        w_ref.at[:, pl.ds(pl.multiple_of((1 - core) * half, LN), half)], w_other, partner
    )
    hdm_in[z] = hdm_out[z]
    gate_t[...] = short(2, q_ref, 0).T
    rows = NB * CW
    x_buf[:, pl.ds(0, rows)] = jnp.zeros((2, rows, LN), F32)
    arrived(m_copies)
    for src in range(NZ):
        for jj in range(2):
            m_buf[pl.ds((2 * src + jj) * CW, CW)] = hdm_in[src, 2, jj].astype(F32)

    def build(channel, carry):
        u_buf[channel] = jnp.concatenate(toeplitz(m_buf, channel), axis=1)
        return carry

    lax.fori_loop(0, CW, build, 0, unroll=BU)

    def load_x(value_of, first):
        for sig in range(2):
            for src in range(NZ):
                for jj in range(2):
                    x_buf[sig, pl.ds(first + (2 * src + jj) * CW, CW)] = value_of(
                        src, jj, sig
                    ).astype(F32)

    def lines_of(channel, first):
        return jnp.concatenate(
            [
                jnp.concatenate(
                    [x_buf[sig, pl.ds(first(k) + channel, NB, stride=CW)] for sig in range(2)],
                    axis=0,
                ).astype(BF)
                for k in range(NB)
            ],
            axis=1,
        )

    def keep_y(channel, value):
        for sig in range(2):
            y_buf[sig, pl.ds(channel, NB, stride=CW)] = value[sig * NB : (sig + 1) * NB]

    def conv(channel, carry):
        left = lines_of(channel, lambda k: (NB - k) * CW)
        pieces = [u_buf[channel, :, pl.ds(LN * k, LN)] for k in range(NB)]
        keep_y(
            channel,
            jnp.dot(left, jnp.concatenate(pieces, axis=0), preferred_element_type=F32),
        )
        return carry

    def corr(channel, carry):
        left = lines_of(channel, lambda k: k * CW)
        keep_y(
            channel,
            lax.dot_general(
                left, u_buf[channel], (((1,), (1,)), ((), ())), preferred_element_type=F32
            ),
        )
        return carry

    arrived(hd_copies)
    load_x(lambda src, jj, sig: hdm_in[src, sig, jj], rows)
    conv_copies = [[] for _ in range(NP)]
    for g in range(NG):
        lax.fori_loop(g * GW, (g + 1) * GW, conv, 0, unroll=CU)
        for jj in range(NP):
            for dest in range(NZ):
                for sig in range(2):
                    conv_out[dest, g, jj, sig] = y_buf[
                        sig, pl.ds((2 * dest + jj) * CW + g * GW, GW)
                    ].astype(BF)
        for jj in range(NP):
            conv_copies[jj] += exchange(
                lambda to, g=g, jj=jj: conv_out.at[to, g, jj],
                lambda me, g=g, jj=jj: conv_in.at[me, g, jj],
            )
    conv_in[z] = conv_out[z]

    pairs = []
    for t in range(NP):
        arrived(conv_copies[t])
        for sig in range(2):
            gated = conv_in[:, :, t, sig].astype(F32).reshape(BL, LN) * gate_t[:, t * LN : (t + 1) * LN]
            own[t, pl.ds(sig * LN, LN)] = gated.T.astype(BF)
        pairs.append(cp.start(own.at[t], other.at[t], partner))
    loads[0].wait()
    w_copy.wait_recv()
    parts = (part_a, part_b)
    crossing = [(part_a, cot_a, True), (part_b, cot_b, False)]

    def product(t, r, dest):
        part = parts[r]
        line = pl.ds(r * LN, LN)

        def one(e, carry):
            block = dest * NR + e if r == 0 else e * NR + dest
            columns = pl.ds(pl.multiple_of(block * BL, BL), BL)
            part[t, dest, e] = (
                jnp.dot(own[t, line], w_own[:, columns], preferred_element_type=F32)
                + jnp.dot(other[t, line], w_other[:, columns], preferred_element_type=F32)
            ).astype(BF)
            return carry

        lax.fori_loop(0, NR, one, 0, unroll=True)

    def products(t, o):
        for r in range(2):
            product(t, r, place(r == 0, o))

    class Scatter:
        def __init__(self, halves, relays, landings, first):
            self.halves, self.relays, self.landings = halves, relays, landings
            self.axes = [first, not first]
            self.far, self.rest = [[], []], [[], []]

        def send_far(self, r):
            a = self.axes[r]
            for side in range(2):
                self.far[r].append(
                    cp.start(
                        self.halves(r, place(a, 2), side),
                        self.relays.at[r, side],
                        ahead(a, (1, 3)[side]),
                    )
                )

        def send_near(self, r, side):
            a, o = self.axes[r], (1, 3)[side]
            self.rest[r].append(
                cp.start(
                    self.halves(r, place(a, o), 1 - side),
                    self.landings.at[r, side, 1 - side],
                    ahead(a, o),
                )
            )

        def pass_on(self):
            for side in range(2):
                for r in range(2):
                    a, o = self.axes[r], (1, 3)[side]
                    self.far[r][side].wait_recv()
                    chunk = self.halves(r, place(a, o), side)
                    chunk[...] = (
                        chunk[...].astype(F32) + self.relays[r, side].astype(F32)
                    ).astype(BF)
                    self.rest[r].append(
                        cp.start(chunk, self.landings.at[r, side, side], ahead(a, o))
                    )

        def wait(self):
            for r in range(2):
                arrived(self.rest[r])

        def start(self):
            for r in range(2):
                self.send_far(r)
            for r in range(2):
                for side in range(2):
                    self.send_near(r, side)

    wide = [
        Scatter(
            lambda r, q, h, t=t: parts[r].at[t, q, pl.ds(2 * h, 2)],
            relay.at[t],
            landed.at[t],
            True,
        )
        for t in range(NP)
    ]
    narrow = [
        Scatter(
            lambda r, q, h, t=t: second.at[t, r, q, pl.ds(h * LN // 2, LN // 2)],
            relay2.at[t],
            landed2.at[t],
            False,
        )
        for t in range(NP)
    ]

    def finish_wide(t):
        wide[t].wait()
        for r in range(2):
            me = (x, y)[r]
            for e in range(NR):
                second[t, r, e] = (
                    parts[r][t, me, e].astype(F32)
                    + landed[t, r, 0, e // 2, e % 2].astype(F32)
                    + landed[t, r, 1, e // 2, e % 2].astype(F32)
                ).astype(BF)
        narrow[t].start()

    class Gather:
        def __init__(self, t, stage):
            self.t, self.stage, self.kept = t, stage, [[], []]

        def half_at(self, r, o, h):
            slot = place((r == 0) == (self.stage == 1), o)
            ref = (cot_a, cot_b)[r]
            if self.stage == 0:
                return ref.at[self.t, (x, y)[r], slot, pl.ds(h * LN, LN)]
            return ref.at[self.t, slot, pl.ds(2 * h, 2)]

        def send(self, r, o, h, side):
            along_x = (r == 0) == (self.stage == 1)
            ref = self.half_at(r, o, h)
            self.kept[r].append(cp.start(ref, ref, ahead(along_x, (1, 3)[side])))

        def start(self):
            for r in range(2):
                self.send(r, 0, 0, 0)
                self.send(r, 0, 1, 1)
            for r in range(2):
                self.send(r, 0, 1, 0)
                self.send(r, 0, 0, 1)

        def pass_on(self):
            for r in range(2):
                self.kept[r][0].wait_recv()
                self.send(r, 3, 0, 0)
                self.kept[r][1].wait_recv()
                self.send(r, 1, 1, 1)

        def wait(self):
            for r in range(2):
                arrived(self.kept[r][2:])

    gathers = [[Gather(t, stage) for stage in range(2)] for t in range(NP)]
    scaling = 1.0 / math.sqrt(NZ * BL)

    def cotangents(t):
        narrow[t].wait()
        sums = [
            second[t, r, (y, x)[r]].astype(F32)
            + landed2[t, r, 0].astype(F32).reshape(LN, BL)
            + landed2[t, r, 1].astype(F32).reshape(LN, BL)
            for r in range(2)
        ]
        bent = jnp.tanh(sums[0] - goal[pl.ds(t * LN, LN)].astype(F32))
        cot_a[t, x, y] = (scaling * bent).T.astype(BF)
        cot_b[t, y, x] = (scaling * (1.0 - bent * bent) * sums[1]).T.astype(BF)
        gathers[t][0].start()

    def widen(t):
        gathers[t][0].wait()
        gathers[t][1].start()

    swaps = [None] * NP

    def back(t):
        gathers[t][1].wait()
        acc[t] = jnp.zeros_like(acc[t])

        def one(q, carry):
            for side, w in enumerate((w_own, w_other)):
                total = None
                for e in range(NR):
                    right = jnp.concatenate([cot_a[t, q, e], cot_b[t, e, q]], axis=1)
                    columns = pl.ds(pl.multiple_of((q * NR + e) * BL, BL), BL)
                    term = jnp.dot(w[:, columns], right, preferred_element_type=F32)
                    total = term if total is None else total + term
                acc[t, side] += total
            return carry

        lax.fori_loop(0, NR, one, 0, unroll=True)
        swaps[t] = cp.start(acc.at[t, 1], acc_in.at[t], partner)

    dz_copies = []

    def send_dz(t):
        swaps[t].wait_recv()
        for sig in range(2):
            lanes = slice(sig * LN, (sig + 1) * LN)
            dz = gate_t[:, t * LN : (t + 1) * LN] * (acc[t, 0, :, lanes] + acc_in[t, :, lanes])
            dz_out[:, t, sig] = dz.reshape(NZ, CW, LN).astype(BF)
        dz_copies.extend(exchange(lambda to: dz_out.at[to, t], lambda me: dz_in.at[me, t]))

    pairs[0].wait_recv()
    products(0, 2)
    for r in range(2):
        wide[0].send_far(r)
    products(0, 1)
    for r in range(2):
        wide[0].send_near(r, 0)
    products(0, 3)
    for r in range(2):
        wide[0].send_near(r, 1)
    products(0, 0)
    pairs[1].wait_recv()
    products(1, 2)
    wide[0].pass_on()
    for r in range(2):
        wide[1].send_far(r)
    products(1, 1)
    products(1, 3)
    for r in range(2):
        for side in range(2):
            wide[1].send_near(r, side)
    products(1, 0)
    finish_wide(0)
    wide[1].pass_on()
    narrow[0].pass_on()
    loads[1].wait()
    cotangents(0)
    finish_wide(1)
    gathers[0][0].pass_on()
    narrow[1].pass_on()
    widen(0)
    cotangents(1)
    gathers[1][0].pass_on()
    gathers[0][1].pass_on()
    widen(1)
    back(0)
    gathers[1][1].pass_on()
    send_dz(0)
    back(1)
    x_buf[:, pl.ds(rows, rows)] = jnp.zeros((2, rows, LN), F32)
    send_dz(1)
    dz_in[z] = dz_out[z]
    arrived(dz_copies)

    load_x(lambda src, jj, sig: dz_in[src, jj, sig], 0)
    res_copies = []
    for g in range(NG):
        lax.fori_loop(g * GW, (g + 1) * GW, corr, 0, unroll=CU)
        for dest in range(NZ):
            for jj in range(2):
                for sig in range(2):
                    res_out[dest, g, jj, sig] = y_buf[
                        sig, pl.ds((2 * dest + jj) * CW + g * GW, GW)
                    ].astype(BF)
        res_copies += exchange(
            lambda to, g=g: res_out.at[to, g], lambda me, g=g: res_in.at[me, g]
        )
    res_in[z] = res_out[z]
    arrived(res_copies)
    res_ref[...] = res_in[...]
    cp.drain()


def products_of_a_step(q, k, v, taps, h, d, w, target):
    half = w.shape[1] // 2
    rows = NB * CW
    hdm = (NZ, 3, 2, CW, LN)
    groups = (NZ, NG, NP, 2, GW, LN)
    plain = (NZ, NP, 2, CW, LN)
    return pl.pallas_call(
        kernel,
        out_shape=jax.ShapeDtypeStruct(groups, BF),
        in_specs=[VM] * 6 + [ANY, ANY],
        out_specs=VM,
        scratch_shapes=[
            pltpu.VMEM((3, 16, BL), BF),
            pltpu.VMEM((3, BL + 16, BL), F32),
            pltpu.VMEM((BL, BL), F32),
            pltpu.VMEM(hdm, BF),
            pltpu.VMEM(hdm, BF),
            pltpu.VMEM((rows, LN), F32),
            pltpu.VMEM((2, 2 * rows, LN), F32),
            pltpu.VMEM((2, rows, LN), F32),
            pltpu.VMEM((CW, LN, NB * LN), BF),
            pltpu.VMEM(groups, BF),
            pltpu.VMEM(groups, BF),
            pltpu.VMEM((NP, BL, BL), BF),
            pltpu.VMEM((NP, BL, BL), BF),
            pltpu.VMEM((BL, half), BF),
            pltpu.VMEM((BL, half), BF),
            pltpu.VMEM((BL, BL), BF),
            pltpu.VMEM((NP, NR, NR, LN, BL), BF),
            pltpu.VMEM((NP, NR, NR, LN, BL), BF),
            pltpu.VMEM((NP, 2, 2, 2, LN, BL), BF),
            pltpu.VMEM((NP, 2, 2, 2, 2, LN, BL), BF),
            pltpu.VMEM((NP, 2, NR, LN, BL), BF),
            pltpu.VMEM((NP, 2, 2, LN // 2, BL), BF),
            pltpu.VMEM((NP, 2, 2, 2, LN // 2, BL), BF),
            pltpu.VMEM((NP, NR, NR, BL, LN), BF),
            pltpu.VMEM((NP, NR, NR, BL, LN), BF),
            pltpu.VMEM((NP, 2, BL, BL), F32),
            pltpu.VMEM((NP, BL, BL), F32),
            pltpu.VMEM(plain, BF),
            pltpu.VMEM(plain, BF),
            pltpu.VMEM(groups, BF),
            pltpu.VMEM(groups, BF),
            pltpu.SemaphoreType.DMA((2,)),
            pltpu.SemaphoreType.DMA((N_COPIES,)),
            pltpu.SemaphoreType.DMA((N_COPIES,)),
        ],
        compiler_params=pltpu.CompilerParams(
            collective_id=0, has_side_effects=True, vmem_limit_bytes=60 * 2**20
        ),
        name="step",
    )(q, k, v, taps, h, d, w, target)


def unfold_kernel(src_ref, a_ref, b_ref):
    for sig, ref in enumerate((a_ref, b_ref)):
        for jj in range(2):
            ref[pl.ds(jj * LN, LN)] = src_ref[:, :, jj, sig].astype(F32).reshape(BL, LN).T


def unfold(src):
    return pl.pallas_call(
        unfold_kernel,
        out_shape=(jax.ShapeDtypeStruct((BL, BL), F32),) * 2,
        in_specs=[VM],
        out_specs=(VM, VM),
        name="unfold",
    )(src)


def on_device(*args):
    return unfold(products_of_a_step(*args))


def solution(mesh):
    in_specs = (
        P("ctx", "chan"),
        P("ctx", "chan"),
        P("ctx", "chan"),
        P(None, None, "chan"),
        P("ctx", "chan"),
        P("ctx", "chan"),
        P("chan", None),
        P("ctx", None),
    )
    out_specs = (P("ctx", "chan"), P("ctx", "chan"))
    return jax.shard_map(
        on_device, mesh=mesh, in_specs=in_specs, out_specs=out_specs, check_vma=False
    )
```
